32 devices in a mesh: layer: 32 (over z, y, x, core).
Axes of the slice: x: 2, y: 2, z: 4, core: 2. Of those that a mesh axis runs over, the one named last changes fastest.
Arguments:
- lower_block: float32 [32, 512, 512], P('layer'), may hold values from -0.109375 to 0.109375
- upper_block: float32 [32, 512, 512], P('layer'), may hold values from -0.109375 to 0.109375
- right_side: float32 [32, 64, 512], P('layer'), may hold values from -6 to 6
Outputs:
- reduced_lower: float32 [32, 512, 512], P('layer')
- reduced_upper: float32 [32, 512, 512], P('layer')
- reduced_rhs: float32 [32, 64, 512], P('layer')
The draws below stay inside these ranges and needn't reach their ends.
All inputs are finite; a program needn't handle non-finite values.
Results may differ from the reference program's by a relative error of at most 0.00022.
Values sent between devices are 32-bit elements; how exact they have to be, the bound alone decides.
A program may use at most 64 MiB of HBM per device.

```python
import math
import jax
import jax.numpy as jnp
from jax import lax

BLOCK = 512
COLUMNS = 64
LEVELS = 3
CHAINS = 8
LAYERS = 32


def block_scale(key, dims, shards, low, largest):
    level, own = 1.0, jax.random.fold_in(key, 6)
    for axis_at, blocks in shards:
        draws = jnp.exp(jax.random.uniform(jax.random.fold_in(own, axis_at), (blocks,), jnp.float32, low / len(shards), largest / len(shards)))
        level = level * jnp.repeat(draws, dims[axis_at] // blocks).reshape([-1 if axis == axis_at else 1 for axis in range(len(dims))])
    return level


def normal_values(key, dims, deviation, bound, pieces=(), kind=jnp.bfloat16):
    factor_of = block_scale(key, dims, pieces, -0.22, 0.18) if pieces else 1.0
    drawn = jax.random.normal(key, dims, jnp.float32) * deviation * factor_of
    return jnp.minimum(jnp.maximum(drawn, -bound), bound).astype(kind)


def setup_inputs(seed: int = 0) -> dict:
    key_list = jax.random.split(jax.random.key(seed), 4)
    lower_block = normal_values(key_list[0], (LAYERS, BLOCK, BLOCK), (6 * BLOCK) ** -0.5, 0.109375, ((0, 32),), jnp.float32)
    upper_block = normal_values(key_list[1], (LAYERS, BLOCK, BLOCK), (6 * BLOCK) ** -0.5, 0.109375, ((0, 32),), jnp.float32)
    right_side = normal_values(key_list[2], (LAYERS, COLUMNS, BLOCK), 1.0, 6.0, ((0, 32),), jnp.float32)
    return dict(lower_block=lower_block, upper_block=upper_block, right_side=right_side)


def matmul_high(left, right):
    return jnp.dot(left, right, precision=lax.Precision.HIGHEST, preferred_element_type=jnp.float32)

def rows_times(block, columns):
    return lax.dot_general(columns, block, (((1,), (1,)), ((), ())), precision=lax.Precision.HIGHEST, preferred_element_type=jnp.float32)

def reduce_level(group):
    own, from_below, from_above = group
    own_lower = own[:BLOCK]
    own_upper = own[BLOCK:2 * BLOCK]
    own_rhs = own[2 * BLOCK:]
    identity = jnp.eye(BLOCK, dtype=jnp.float32)
    diagonal = identity - matmul_high(own_lower, from_below[BLOCK:2 * BLOCK]) - matmul_high(own_upper, from_above[:BLOCK])
    initial = 2.0 * identity - diagonal
    inverse = matmul_high(initial, 2.0 * identity - matmul_high(diagonal, initial))
    new_lower = -matmul_high(inverse, matmul_high(own_lower, from_below[:BLOCK]))
    new_upper = -matmul_high(inverse, matmul_high(own_upper, from_above[BLOCK:2 * BLOCK]))
    new_rhs = own_rhs - rows_times(own_lower, from_below[2 * BLOCK:]) - rows_times(own_upper, from_above[2 * BLOCK:])
    new_rhs = rows_times(inverse, new_rhs)
    return jnp.concatenate([new_lower, new_upper, new_rhs], axis=0)

def reference(lower_block, upper_block, right_side):
    layers = lower_block.shape[0]
    payload = jnp.concatenate([lower_block, upper_block, right_side], axis=1)
    for level_index in range(LEVELS):
        stride = 2 ** level_index
        from_below = jnp.roll(payload, stride, axis=0)
        from_above = jnp.roll(payload, -stride, axis=0)
        payload = lax.map(reduce_level, (payload, from_below, from_above))
    chain_len = layers // CHAINS
    payload = payload.reshape(chain_len, CHAINS, payload.shape[1], payload.shape[2])
    payload = jnp.transpose(payload, (1, 0, 2, 3)).reshape(layers, payload.shape[2], payload.shape[3])
    factor = 2.5 ** 8 * math.sqrt(BLOCK)
    return (payload[:, :BLOCK] * factor, payload[:, BLOCK:2 * BLOCK] * factor, payload[:, 2 * BLOCK:])
```

```python
import functools
import math

import jax
import jax.numpy as jnp
from jax import lax
from jax.experimental import pallas as pl
from jax.experimental.pallas import tpu as pltpu
from jax.sharding import PartitionSpec as P

LEVELS = 3
CHAINS = 8
PER = 4
F32, BF16 = jnp.float32, jnp.bfloat16
MESH = pl.DeviceIdType.MESH


def halves(value):
    high = value.astype(BF16)
    return high, (value - high.astype(F32)).astype(BF16)


def dot3(a_high, a_low, b_high, b_low, transposed=False):
    dims = (((1,), (1 if transposed else 0,)), ((), ()))
    dot = lambda a, b: lax.dot_general(a, b, dims, preferred_element_type=F32)
    return dot(a_high, b_high) + (dot(a_high, b_low) + dot(a_low, b_high))


def placements(n):
    planes = n // CHAINS
    quarter = planes // 4

    def parts(layer):
        j, r = layer // CHAINS, layer % CHAINS
        return j // (2 * quarter), (j // 2) % quarter, j % 2, r // 4, (r // 2) % 2, r % 2

    def join(b4, mid, b3, b2, b1, b0):
        return CHAINS * (b4 * 2 * quarter + mid * 2 + b3) + 4 * b2 + 2 * b1 + b0

    def middle(layer):
        b4, mid, b3, b2, b1, b0 = parts(layer)
        return 8 * ((b0 * 2 + b4) * quarter + mid) + 4 * b2 + 2 * ((b4 + b3) % 2) + b1

    def middle_layer(dev):
        z, y, x, core = dev // 8, (dev // 4) % 2, (dev // 2) % 2, dev % 2
        b0, b4, mid = z // (2 * quarter), (z // quarter) % 2, z % quarter
        return join(b4, mid, (x + b4) % 2, y, core, b0)

    def last(layer):
        b4, mid, b3, b2, b1, b0 = parts(layer)
        return 8 * ((b0 * 2 + b4) * quarter + mid) + 4 * ((b1 + b0) % 2) + 2 * ((b4 + b3) % 2) + b2

    def last_layer(dev):
        z, y, x, core = dev // 8, (dev // 4) % 2, (dev // 2) % 2, dev % 2
        b0, b4, mid = z // (2 * quarter), (z // quarter) % 2, z % quarter
        return join(b4, mid, (x + b4) % 2, core, (y + b0) % 2, b0)

    def regrouped(layer):
        return (layer % CHAINS) * planes + layer // CHAINS

    def regrouped_layer(dev):
        return (dev % planes) * CHAINS + dev // planes

    same = lambda at: at
    return (same, middle, last, regrouped), (same, middle_layer, last_layer, regrouped_layer)


def kernel(n, order, columns, factor, lower_ref, upper_ref, rhs_ref, out_lower, out_upper, out_rhs,
           bufs, fin, acc, ush, usl, lsh, lsl, uah, ual, lah, lal, ubh, ubl, lbh, lbl,
           eh, el, qh, ql, yh, yl, uxh, uxl, lxh, lxl,
           load_sem, send_sem, recv_sem, fin_send, fin_recv):
    me = lax.axis_index("layer")
    core = me % 2
    mate = me + 1 - 2 * core
    half = order // 2
    size = order // PER
    tail = 2 * PER
    device_of, layer_of = placements(n)

    partner, target, source = [], [None], [None]
    for level in range(LEVELS):
        stride = 1 << level
        mine = layer_of[level](me)
        partner.append(device_of[level]((mine + stride * (2 * core - 1) + n) % n))
        target.append(device_of[level + 1](mine))
        source.append(device_of[level](layer_of[level + 1](me)))
    goes_to, comes_from = target[LEVELS], source[LEVELS]
    moves = goes_to != me

    def rows_of(piece):
        if isinstance(piece, int) and piece == tail:
            return pl.ds(2 * order, columns)
        return pl.ds(pl.multiple_of(piece * size, size), size)

    def remote(level, from_slot, to_slot, flow, piece, dev):
        return pltpu.make_async_remote_copy(
            src_ref=bufs.at[level, from_slot, rows_of(piece)],
            dst_ref=bufs.at[level, to_slot, rows_of(piece)],
            send_sem=send_sem.at[level, flow, piece],
            recv_sem=recv_sem.at[level, to_slot - 1, piece],
            device_id=(dev,),
            device_id_type=MESH,
        )

    def hand_on(level, slot, piece):
        remote(level, slot, 3, 2, piece, partner[level]).start()
        remote(level, slot, 2, 1, piece, mate).start()

    def send_own(level, piece):
        @pl.when(target[level] != me)
        def _():
            remote(level, 0, 1, 0, piece, target[level]).start()

        @pl.when(target[level] == me)
        def _():
            hand_on(level, 0, piece)

    barrier = pltpu.get_barrier_semaphore()

    def greet(dev):
        pl.semaphore_signal(barrier, inc=1, device_id=(dev,), device_id_type=MESH)

    loads = []
    for index, (ref, start, count) in enumerate(((upper_ref, 0, order), (lower_ref, order, order), (rhs_ref, 2 * order, columns))):
        copy = pltpu.make_async_copy(ref.at[0], bufs.at[0, 0, pl.ds(start, count)], load_sem.at[index])
        copy.start()
        loads.append(copy)

    greet(mate)
    expected = jnp.int32(1 + LEVELS)
    for level in range(LEVELS):
        greet(partner[level])
    for level in range(1, LEVELS + 1):
        @pl.when(source[level] != me)
        def _():
            greet(source[level])

        expected += (target[level] != me).astype(jnp.int32)
    pl.semaphore_wait(barrier, expected)

    for copy in loads:
        copy.wait()
    for piece in range(tail + 1):
        hand_on(0, 0, piece)

    def block(r):
        return pl.ds(pl.multiple_of(r * half, half), half)

    def split(level, slot, piece, at, high_ref, low_ref):
        high, low = halves(bufs[level, slot, rows_of(piece), :])
        rows = pl.ds(pl.multiple_of(at * size, size), size)
        high_ref[rows, :] = high
        low_ref[rows, :] = low

    def store(high_ref, low_ref, rows, value):
        high, low = halves(value)
        high_ref[rows, :] = high
        low_ref[rows, :] = low


    def fin_copy(piece, out, out_rows):
        return pltpu.make_async_remote_copy(
            src_ref=fin.at[rows_of(piece)], dst_ref=out.at[0, out_rows],
            send_sem=fin_send.at[piece], recv_sem=fin_recv.at[piece],
            device_id=(goes_to,), device_id_type=MESH)

    def fin_local(piece, out, out_rows):
        return pltpu.make_async_copy(fin.at[rows_of(piece)], out.at[0, out_rows], load_sem.at[piece])

    def send_fin(piece, out, out_rows):
        @pl.when(moves)
        def _():
            fin_copy(piece, out, out_rows).start()

        @pl.when(jnp.logical_not(moves))
        def _():
            fin_local(piece, out, out_rows).start()

    for level in range(LEVELS):
        if level:
            moved = source[level] != me
            self_slot = jnp.where(moved, 1, 0)
        else:
            moved, self_slot = None, 0
        above = 2 + core
        below = 3 - core

        def take_self(piece):
            if moved is not None:
                @pl.when(moved)
                def _():
                    remote(level, 0, 1, 0, piece, mate).wait_recv()
                    hand_on(level, 1, piece)

        def take_others(piece):
            remote(level, 0, 2, 0, piece, mate).wait_recv()
            remote(level, 0, 3, 0, piece, mate).wait_recv()

        take_self(0)

        @pl.loop(0, PER)
        def _(piece):
            take_self(piece + 1)
            split(level, self_slot, piece, piece, ush, usl)
            take_others(piece)
            split(level, above, piece, piece, uah, ual)
            split(level, below, piece, piece, ubh, ubl)

        @pl.loop(0, 2)
        def _(r):
            store(uxh, uxl, block(r), dot3(ush[block(r), :], usl[block(r), :], uah[...], ual[...]))

        for k in range(2):
            @pl.loop(k * (PER // 2), (k + 1) * (PER // 2))
            def _(at):
                piece = PER + at

                @pl.when(at + 1 < PER)
                def _():
                    take_self(piece + 1)

                split(level, self_slot, piece, at, lsh, lsl)
                take_others(piece)
                split(level, above, piece, at, lah, lal)
                split(level, below, piece, at, lbh, lbl)

            part = pl.ds(k * half, half)
            for r in range(2):
                rows = pl.ds(r * half, half)
                value = dot3(ush[rows, part], usl[rows, part], lah[part, :], lal[part, :])
                if r == k:
                    value = value + dot3(lsh[rows, :], lsl[rows, :], ubh[...], ubl[...])
                if k == 0:
                    acc[rows, :] = value
                else:
                    store(eh, el, rows, acc[rows, :] + value)

        @pl.loop(0, 2)
        def _(r):
            store(qh, ql, block(r), dot3(eh[block(r), :], el[block(r), :], eh[...], el[...]))

        def emit(which, r, high_ref, low_ref):
            value = dot3(yh[block(r), :], yl[block(r), :], high_ref[...], low_ref[...])
            rows = pl.ds(pl.multiple_of(which * order + r * half, half), half)
            if level < LEVELS - 1:
                bufs[level + 1, 0, rows, :] = -value
            else:
                fin[rows, :] = value * (-factor)
            for t in range(PER // 2):
                at = r * (PER // 2) + t
                if level < LEVELS - 1:
                    send_own(level + 1, which * PER + at)
                else:
                    out_rows = pl.ds(pl.multiple_of(at * size, size), size)
                    send_fin(which * PER + at, out_lower if which else out_upper, out_rows)

        @pl.loop(0, 2)
        def _(r):
            rows = lax.broadcasted_iota(jnp.int32, (half, order), 0) + r * half
            cols = lax.broadcasted_iota(jnp.int32, (half, order), 1)
            eye = jnp.where(rows == cols, 1.0, 0.0).astype(F32)
            value = dot3(eh[block(r), :], el[block(r), :], qh[...], ql[...])
            e = eh[block(r), :].astype(F32) + el[block(r), :].astype(F32)
            q = qh[block(r), :].astype(F32) + ql[block(r), :].astype(F32)
            store(yh, yl, block(r), eye + (e + (q + value)))
            emit(0, r, uxh, uxl)

        take_self(tail)

        @pl.loop(0, 2)
        def _(r):
            store(lxh, lxl, block(r), dot3(lsh[block(r), :], lsl[block(r), :], lbh[...], lbl[...]))

        @pl.loop(0, 2)
        def _(r):
            emit(1, r, lxh, lxl)

        take_others(tail)
        below_high, below_low = halves(bufs[level, below, rows_of(tail), :])
        above_high, above_low = halves(bufs[level, above, rows_of(tail), :])
        right = (bufs[level, self_slot, rows_of(tail), :]
                 - dot3(below_high, below_low, lsh[...], lsl[...], True)
                 - dot3(above_high, above_low, ush[...], usl[...], True))
        right_high, right_low = halves(right)
        right = dot3(right_high, right_low, yh[...], yl[...], True)
        if level < LEVELS - 1:
            bufs[level + 1, 0, rows_of(tail), :] = right
            send_own(level + 1, tail)
        else:
            fin[rows_of(tail), :] = right
            send_fin(tail, out_rhs, pl.ds(0, columns))

    for level in range(LEVELS):
        for piece in range(tail + 1):
            if level:
                @pl.when(target[level] != me)
                def _():
                    remote(level, 0, 1, 0, piece, target[level]).wait_send()
            remote(level, 0, 2, 1, piece, mate).wait_send()
            remote(level, 0, 3, 2, piece, partner[level]).wait_send()

    ends = [(p, out_lower if p >= PER else out_upper, pl.ds((p % PER) * size, size)) for p in range(tail)]
    ends.append((tail, out_rhs, pl.ds(0, columns)))
    for piece, out, out_rows in ends:
        @pl.when(moves)
        def _():
            copy = fin_copy(piece, out, out_rows)
            copy.wait_send()
            copy.wait_recv()

        @pl.when(jnp.logical_not(moves))
        def _():
            fin_local(piece, out, out_rows).wait()


def per_device(lower_block, upper_block, right_side):
    n = lax.axis_size("layer")
    order, columns = lower_block.shape[2], right_side.shape[1]
    rows = 2 * order + columns
    one = lambda: pltpu.VMEM((order, order), BF16)
    pieces = 2 * PER + 1
    return pl.pallas_call(
        functools.partial(kernel, n, order, columns, 2.5**8 * math.sqrt(order)),
        out_shape=[jax.ShapeDtypeStruct(a.shape, F32) for a in (lower_block, upper_block, right_side)],
        in_specs=[pl.BlockSpec(memory_space=pl.ANY)] * 3,
        out_specs=[pl.BlockSpec(memory_space=pltpu.VMEM)] * 3,
        scratch_shapes=[
            pltpu.VMEM((LEVELS, 4, rows, order), F32),
            pltpu.VMEM((rows, order), F32),
            pltpu.VMEM((order, order), F32),
            *[one() for _ in range(22)],
            pltpu.SemaphoreType.DMA((pieces,)),
            pltpu.SemaphoreType.DMA((LEVELS, 3, pieces)),
            pltpu.SemaphoreType.DMA((LEVELS, 3, pieces)),
            pltpu.SemaphoreType.DMA((pieces,)),
            pltpu.SemaphoreType.DMA((pieces,)),
        ],
        compiler_params=pltpu.CompilerParams(
            collective_id=0, has_side_effects=True, vmem_limit_bytes=60 * 1024 * 1024
        ),
    )(lower_block, upper_block, right_side)


def solution(mesh):
    placed = (P("layer", None, None), P("layer", None, None), P("layer", None, None))
    return jax.shard_map(
        per_device,
        mesh=mesh,
        in_specs=placed,
        out_specs=placed,
        check_vma=False,
    )
```

```python
import functools
import math

import jax
import jax.numpy as jnp
from jax import lax
from jax.experimental import pallas as pl
from jax.experimental.pallas import tpu as pltpu
from jax.sharding import PartitionSpec as P

LEVELS = 3
CHAINS = 8
PER = 8
AHEAD = 2
LAG = 2
F32, BF16 = jnp.float32, jnp.bfloat16
MESH = pl.DeviceIdType.MESH


def halves(value):
    high = value.astype(BF16)
    return high, (value - high.astype(F32)).astype(BF16)


def dot3(a_high, a_low, b_high, b_low, transposed=False):
    dims = (((1,), (1 if transposed else 0,)), ((), ()))
    dot = lambda a, b: lax.dot_general(a, b, dims, preferred_element_type=F32)
    return dot(a_high, b_high) + (dot(a_high, b_low) + dot(a_low, b_high))


def placements(n):
    planes = n // CHAINS
    quarter = planes // 4

    def parts(layer):
        j, r = layer // CHAINS, layer % CHAINS
        return j // (2 * quarter), (j // 2) % quarter, j % 2, r // 4, (r // 2) % 2, r % 2

    def join(b4, mid, b3, b2, b1, b0):
        return CHAINS * (b4 * 2 * quarter + mid * 2 + b3) + 4 * b2 + 2 * b1 + b0

    def middle(layer):
        b4, mid, b3, b2, b1, b0 = parts(layer)
        return 8 * ((b0 * 2 + b4) * quarter + mid) + 4 * b2 + 2 * ((b4 + b3) % 2) + b1

    def middle_layer(dev):
        z, y, x, core = dev // 8, (dev // 4) % 2, (dev // 2) % 2, dev % 2
        b0, b4, mid = z // (2 * quarter), (z // quarter) % 2, z % quarter
        return join(b4, mid, (x + b4) % 2, y, core, b0)

    def last(layer):
        b4, mid, b3, b2, b1, b0 = parts(layer)
        return 8 * ((b0 * 2 + b4) * quarter + mid) + 4 * ((b1 + b0) % 2) + 2 * ((b4 + b3) % 2) + b2

    def last_layer(dev):
        z, y, x, core = dev // 8, (dev // 4) % 2, (dev // 2) % 2, dev % 2
        b0, b4, mid = z // (2 * quarter), (z // quarter) % 2, z % quarter
        return join(b4, mid, (x + b4) % 2, core, (y + b0) % 2, b0)

    def regrouped(layer):
        return (layer % CHAINS) * planes + layer // CHAINS

    def regrouped_layer(dev):
        return (dev % planes) * CHAINS + dev // planes

    same = lambda at: at
    return (same, middle, last, regrouped), (same, middle_layer, last_layer, regrouped_layer)


def kernel(n, order, columns, factor, lower_ref, upper_ref, rhs_ref, out_lower, out_upper, out_rhs,
           bufs, fin, acc, ush, usl, lsh, lsl, uah, ual, lah, lal, ubh, ubl, lbh, lbl,
           eh, el, qh, ql, yh, yl, uxh, uxl, lxh, lxl,
           load_sem, send_sem, recv_sem, fin_send, fin_recv):
    me = lax.axis_index("layer")
    core = me % 2
    mate = me + 1 - 2 * core
    half = order // 2
    size = order // PER
    tail = 2 * PER
    device_of, layer_of = placements(n)

    partner, target, source = [], [None], [None]
    for level in range(LEVELS):
        stride = 1 << level
        mine = layer_of[level](me)
        partner.append(device_of[level]((mine + stride * (2 * core - 1) + n) % n))
        target.append(device_of[level + 1](mine))
        source.append(device_of[level](layer_of[level + 1](me)))
    goes_to, comes_from = target[LEVELS], source[LEVELS]
    moves = goes_to != me

    def rows_of(piece):
        if isinstance(piece, int) and piece == tail:
            return pl.ds(2 * order, columns)
        return pl.ds(pl.multiple_of(piece * size, size), size)

    def remote(level, from_slot, to_slot, flow, piece, dev):
        return pltpu.make_async_remote_copy(
            src_ref=bufs.at[level, from_slot, rows_of(piece)],
            dst_ref=bufs.at[level, to_slot, rows_of(piece)],
            send_sem=send_sem.at[level, flow, piece],
            recv_sem=recv_sem.at[level, to_slot - 1, piece],
            device_id=(dev,),
            device_id_type=MESH,
        )

    def hand_on(level, slot, piece):
        remote(level, slot, 3, 2, piece, partner[level]).start()
        remote(level, slot, 2, 1, piece, mate).start()

    def send_own(level, piece):
        @pl.when((target[level] != me) & (piece < AHEAD))
        def _():
            remote(level, 0, 1, 0, piece, target[level]).start()

        @pl.when(target[level] == me)
        def _():
            hand_on(level, 0, piece)

    barrier = pltpu.get_barrier_semaphore()

    def greet(dev):
        pl.semaphore_signal(barrier, inc=1, device_id=(dev,), device_id_type=MESH)

    loads = []
    for index, (ref, start, count) in enumerate(((upper_ref, 0, order), (lower_ref, order, order), (rhs_ref, 2 * order, columns))):
        copy = pltpu.make_async_copy(ref.at[0], bufs.at[0, 0, pl.ds(start, count)], load_sem.at[index])
        copy.start()
        loads.append(copy)

    greet(mate)
    expected = jnp.int32(1 + LEVELS)
    for level in range(LEVELS):
        greet(partner[level])
    for level in range(1, LEVELS + 1):
        @pl.when(source[level] != me)
        def _():
            greet(source[level])

        expected += (target[level] != me).astype(jnp.int32)
    pl.semaphore_wait(barrier, expected)

    for copy in loads:
        copy.wait()
    for piece in range(tail + 1):
        hand_on(0, 0, piece)

    def block(r):
        return pl.ds(pl.multiple_of(r * half, half), half)

    def split(level, slot, piece, at, high_ref, low_ref):
        high, low = halves(bufs[level, slot, rows_of(piece), :])
        rows = pl.ds(pl.multiple_of(at * size, size), size)
        high_ref[rows, :] = high
        low_ref[rows, :] = low

    def store(high_ref, low_ref, rows, value):
        high, low = halves(value)
        high_ref[rows, :] = high
        low_ref[rows, :] = low


    def fin_copy(piece, out, out_rows):
        return pltpu.make_async_remote_copy(
            src_ref=fin.at[rows_of(piece)], dst_ref=out.at[0, out_rows],
            send_sem=fin_send.at[piece], recv_sem=fin_recv.at[piece],
            device_id=(goes_to,), device_id_type=MESH)

    def fin_local(piece, out, out_rows):
        return pltpu.make_async_copy(fin.at[rows_of(piece)], out.at[0, out_rows], load_sem.at[piece])

    def send_fin(piece, out, out_rows):
        @pl.when(moves)
        def _():
            fin_copy(piece, out, out_rows).start()

        @pl.when(jnp.logical_not(moves))
        def _():
            fin_local(piece, out, out_rows).start()

    for level in range(LEVELS):
        if level:
            moved = source[level] != me
            self_slot = jnp.where(moved, 1, 0)
        else:
            moved, self_slot = None, 0
        above = 2 + core
        below = 3 - core

        def take_self(piece):
            if moved is not None:
                @pl.when(moved)
                def _():
                    if piece + AHEAD <= tail:
                        remote(level, 0, 1, 0, piece + AHEAD, target[level]).start()
                    remote(level, 0, 1, 0, piece, mate).wait_recv()
                    hand_on(level, 1, piece)

        def take_others(piece):
            remote(level, 0, 2, 0, piece, mate).wait_recv()
            remote(level, 0, 3, 0, piece, mate).wait_recv()

        def coupling_part(k):
            part = pl.ds(k * half, half)
            for r in range(2):
                rows = pl.ds(r * half, half)
                value = dot3(ush[rows, part], usl[rows, part], lah[part, :], lal[part, :])
                if r == k:
                    value = value + dot3(lsh[rows, :], lsl[rows, :], ubh[...], ubl[...])
                if k == 0:
                    acc[rows, :] = value
                else:
                    store(eh, el, rows, acc[rows, :] + value)

        for step in range(tail + LAG):
            if step <= tail:
                take_self(step)
            piece = step - LAG
            if piece < 0:
                continue
            at = piece % PER
            take_others(piece)
            into = ((ush, usl), (uah, ual), (ubh, ubl)) if piece < PER else ((lsh, lsl), (lah, lal), (lbh, lbl))
            for slot, (high_ref, low_ref) in zip((self_slot, above, below), into):
                split(level, slot, piece, at, high_ref, low_ref)
            if piece == PER - 1:
                @pl.loop(0, 2)
                def _(r):
                    store(uxh, uxl, block(r), dot3(ush[block(r), :], usl[block(r), :], uah[...], ual[...]))

            if piece == PER + PER // 2 - 1:
                coupling_part(0)
            if piece == 2 * PER - 1:
                coupling_part(1)

        @pl.loop(0, 2)
        def _(r):
            store(qh, ql, block(r), dot3(eh[block(r), :], el[block(r), :], eh[...], el[...]))

        def emit(which, r, high_ref, low_ref):
            value = dot3(yh[block(r), :], yl[block(r), :], high_ref[...], low_ref[...])
            rows = pl.ds(pl.multiple_of(which * order + r * half, half), half)
            if level < LEVELS - 1:
                bufs[level + 1, 0, rows, :] = -value
            else:
                fin[rows, :] = value * (-factor)
            for t in range(PER // 2):
                at = r * (PER // 2) + t
                if level < LEVELS - 1:
                    send_own(level + 1, which * PER + at)
                else:
                    out_rows = pl.ds(pl.multiple_of(at * size, size), size)
                    send_fin(which * PER + at, out_lower if which else out_upper, out_rows)

        @pl.loop(0, 2)
        def _(r):
            rows = lax.broadcasted_iota(jnp.int32, (half, order), 0) + r * half
            cols = lax.broadcasted_iota(jnp.int32, (half, order), 1)
            eye = jnp.where(rows == cols, 1.0, 0.0).astype(F32)
            value = dot3(eh[block(r), :], el[block(r), :], qh[...], ql[...])
            e = eh[block(r), :].astype(F32) + el[block(r), :].astype(F32)
            q = qh[block(r), :].astype(F32) + ql[block(r), :].astype(F32)
            store(yh, yl, block(r), eye + (e + (q + value)))
            emit(0, r, uxh, uxl)

        @pl.loop(0, 2)
        def _(r):
            store(lxh, lxl, block(r), dot3(lsh[block(r), :], lsl[block(r), :], lbh[...], lbl[...]))

        @pl.loop(0, 2)
        def _(r):
            emit(1, r, lxh, lxl)

        take_others(tail)
        below_high, below_low = halves(bufs[level, below, rows_of(tail), :])
        above_high, above_low = halves(bufs[level, above, rows_of(tail), :])
        right = (bufs[level, self_slot, rows_of(tail), :]
                 - dot3(below_high, below_low, lsh[...], lsl[...], True)
                 - dot3(above_high, above_low, ush[...], usl[...], True))
        right_high, right_low = halves(right)
        right = dot3(right_high, right_low, yh[...], yl[...], True)
        if level < LEVELS - 1:
            bufs[level + 1, 0, rows_of(tail), :] = right
            send_own(level + 1, tail)
        else:
            fin[rows_of(tail), :] = right
            send_fin(tail, out_rhs, pl.ds(0, columns))

    for level in range(LEVELS):
        for piece in range(tail + 1):
            if level:
                @pl.when(target[level] != me)
                def _():
                    remote(level, 0, 1, 0, piece, target[level]).wait_send()
            remote(level, 0, 2, 1, piece, mate).wait_send()
            remote(level, 0, 3, 2, piece, partner[level]).wait_send()

    ends = [(p, out_lower if p >= PER else out_upper, pl.ds((p % PER) * size, size)) for p in range(tail)]
    ends.append((tail, out_rhs, pl.ds(0, columns)))
    for piece, out, out_rows in ends:
        @pl.when(moves)
        def _():
            copy = fin_copy(piece, out, out_rows)
            copy.wait_send()
            copy.wait_recv()

        @pl.when(jnp.logical_not(moves))
        def _():
            fin_local(piece, out, out_rows).wait()


def per_device(lower_block, upper_block, right_side):
    n = lax.axis_size("layer")
    order, columns = lower_block.shape[2], right_side.shape[1]
    rows = 2 * order + columns
    one = lambda: pltpu.VMEM((order, order), BF16)
    pieces = 2 * PER + 1
    return pl.pallas_call(
        functools.partial(kernel, n, order, columns, 2.5**8 * math.sqrt(order)),
        out_shape=[jax.ShapeDtypeStruct(a.shape, F32) for a in (lower_block, upper_block, right_side)],
        in_specs=[pl.BlockSpec(memory_space=pl.ANY)] * 3,
        out_specs=[pl.BlockSpec(memory_space=pltpu.VMEM)] * 3,
        scratch_shapes=[
            pltpu.VMEM((LEVELS, 4, rows, order), F32),
            pltpu.VMEM((rows, order), F32),
            pltpu.VMEM((order, order), F32),
            *[one() for _ in range(22)],
            pltpu.SemaphoreType.DMA((pieces,)),
            pltpu.SemaphoreType.DMA((LEVELS, 3, pieces)),
            pltpu.SemaphoreType.DMA((LEVELS, 3, pieces)),
            pltpu.SemaphoreType.DMA((pieces,)),
            pltpu.SemaphoreType.DMA((pieces,)),
        ],
        compiler_params=pltpu.CompilerParams(
            collective_id=0, has_side_effects=True, vmem_limit_bytes=60 * 1024 * 1024
        ),
    )(lower_block, upper_block, right_side)


def solution(mesh):
    placed = (P("layer", None, None), P("layer", None, None), P("layer", None, None))
    return jax.shard_map(
        per_device,
        mesh=mesh,
        in_specs=placed,
        out_specs=placed,
        check_vma=False,
    )
```

```python
import functools
import math

import jax
import jax.numpy as jnp
from jax import lax
from jax.experimental import pallas as pl
from jax.experimental.pallas import tpu as pltpu
from jax.sharding import PartitionSpec as P

LEVELS = 3
CHAINS = 8
PER = 8
AHEAD = 2
LAG = 2
F32, BF16 = jnp.float32, jnp.bfloat16
MESH = pl.DeviceIdType.MESH


def halves(value):
    high = value.astype(BF16)
    return high, (value - high.astype(F32)).astype(BF16)


def dot3(a_high, a_low, b_high, b_low, transposed=False):
    dims = (((1,), (1 if transposed else 0,)), ((), ()))
    dot = lambda a, b: lax.dot_general(a, b, dims, preferred_element_type=F32)
    return dot(a_high, b_high) + (dot(a_high, b_low) + dot(a_low, b_high))


def placements(n):
    planes = n // CHAINS
    quarter = planes // 4

    def parts(layer):
        j, r = layer // CHAINS, layer % CHAINS
        return j // (2 * quarter), (j // 2) % quarter, j % 2, r // 4, (r // 2) % 2, r % 2

    def join(b4, mid, b3, b2, b1, b0):
        return CHAINS * (b4 * 2 * quarter + mid * 2 + b3) + 4 * b2 + 2 * b1 + b0

    def middle(layer):
        b4, mid, b3, b2, b1, b0 = parts(layer)
        return 8 * ((b0 * 2 + b4) * quarter + mid) + 4 * b2 + 2 * ((b4 + b3) % 2) + b1

    def middle_layer(dev):
        z, y, x, core = dev // 8, (dev // 4) % 2, (dev // 2) % 2, dev % 2
        b0, b4, mid = z // (2 * quarter), (z // quarter) % 2, z % quarter
        return join(b4, mid, (x + b4) % 2, y, core, b0)

    def last(layer):
        b4, mid, b3, b2, b1, b0 = parts(layer)
        return 8 * ((b0 * 2 + b4) * quarter + mid) + 4 * ((b1 + b0) % 2) + 2 * ((b4 + b3) % 2) + b2

    def last_layer(dev):
        z, y, x, core = dev // 8, (dev // 4) % 2, (dev // 2) % 2, dev % 2
        b0, b4, mid = z // (2 * quarter), (z // quarter) % 2, z % quarter
        return join(b4, mid, (x + b4) % 2, core, (y + b0) % 2, b0)

    def regrouped(layer):
        return (layer % CHAINS) * planes + layer // CHAINS

    def regrouped_layer(dev):
        return (dev % planes) * CHAINS + dev // planes

    same = lambda at: at
    return (same, middle, last, regrouped), (same, middle_layer, last_layer, regrouped_layer)


def kernel(n, order, columns, factor, lower_ref, upper_ref, rhs_ref, out_lower, out_upper, out_rhs,
           bufs, fin, acc, part, xh, xl, s1h, s1l, s2h, s2l, n1h, n1l, n2h, n2l, f1h, f1l, f2h, f2l,
           eh, el, qh, ql, yh, yl,
           load_sem, send_sem, recv_sem, fin_send, fin_recv):
    me = lax.axis_index("layer")
    core = me % 2
    mate = me + 1 - 2 * core
    half = order // 2
    size = order // PER
    tail = 2 * PER
    device_of, layer_of = placements(n)

    partner, target, source = [], [None], [None]
    for level in range(LEVELS):
        stride = 1 << level
        mine = layer_of[level](me)
        partner.append(device_of[level]((mine + stride * (2 * core - 1) + n) % n))
        target.append(device_of[level + 1](mine))
        source.append(device_of[level](layer_of[level + 1](me)))
    goes_to, comes_from = target[LEVELS], source[LEVELS]
    moves = goes_to != me

    def rows_of(piece, first):
        if isinstance(piece, int) and piece == tail:
            return pl.ds(2 * order, columns)
        which = (piece // PER + first) % 2
        return pl.ds(pl.multiple_of(which * order + (piece % PER) * size, size), size)

    def remote(level, from_slot, to_slot, flow, piece, first, dev):
        return pltpu.make_async_remote_copy(
            src_ref=bufs.at[level, from_slot, rows_of(piece, first)],
            dst_ref=bufs.at[level, to_slot, rows_of(piece, first)],
            send_sem=send_sem.at[level, flow, piece],
            recv_sem=recv_sem.at[level, to_slot - 1, piece],
            device_id=(dev,),
            device_id_type=MESH,
        )

    def hand_on(level, slot, piece):
        remote(level, slot, 3, 2, piece, 1 - core, partner[level]).start()
        remote(level, slot, 2, 1, piece, 1 - core, mate).start()

    def start_own(level, piece):
        remote(level, 0, 1, 0, piece, 1 - target[level] % 2, target[level]).start()

    def send_own(level, piece):
        @pl.when((target[level] != me) & (piece < AHEAD))
        def _():
            start_own(level, piece)

        @pl.when(target[level] == me)
        def _():
            hand_on(level, 0, piece)

    barrier = pltpu.get_barrier_semaphore()

    def greet(dev):
        pl.semaphore_signal(barrier, inc=1, device_id=(dev,), device_id_type=MESH)

    loads = []
    for index, (ref, start, count) in enumerate(((upper_ref, 0, order), (lower_ref, order, order), (rhs_ref, 2 * order, columns))):
        copy = pltpu.make_async_copy(ref.at[0], bufs.at[0, 0, pl.ds(start, count)], load_sem.at[index])
        copy.start()
        loads.append(copy)

    greet(mate)
    expected = jnp.int32(1 + LEVELS)
    for level in range(LEVELS):
        greet(partner[level])
    for level in range(1, LEVELS + 1):
        @pl.when(source[level] != me)
        def _():
            greet(source[level])

        expected += (target[level] != me).astype(jnp.int32)
    pl.semaphore_wait(barrier, expected)

    for copy in loads:
        copy.wait()
    for piece in range(tail + 1):
        hand_on(0, 0, piece)

    def block(r):
        return pl.ds(pl.multiple_of(r * half, half), half)

    def split(level, slot, piece, first, high_ref, low_ref):
        high, low = halves(bufs[level, slot, rows_of(piece, first), :])
        rows = pl.ds((piece % PER) * size, size)
        high_ref[rows, :] = high
        low_ref[rows, :] = low

    def store(high_ref, low_ref, rows, value):
        high, low = halves(value)
        high_ref[rows, :] = high
        low_ref[rows, :] = low


    def fin_copy(piece, out, out_rows):
        return pltpu.make_async_remote_copy(
            src_ref=fin.at[rows_of(piece, 0)], dst_ref=out.at[0, out_rows],
            send_sem=fin_send.at[piece], recv_sem=fin_recv.at[piece],
            device_id=(goes_to,), device_id_type=MESH)

    def fin_local(piece, out, out_rows):
        return pltpu.make_async_copy(fin.at[rows_of(piece, 0)], out.at[0, out_rows], load_sem.at[piece])

    def send_fin(piece, out, out_rows):
        @pl.when(moves)
        def _():
            fin_copy(piece, out, out_rows).start()

        @pl.when(jnp.logical_not(moves))
        def _():
            fin_local(piece, out, out_rows).start()

    for level in range(LEVELS):
        if level:
            moved = source[level] != me
            self_slot = jnp.where(moved, 1, 0)
        else:
            moved, self_slot = None, 0
        order_next = 1 - target[level + 1] % 2 if level < LEVELS - 1 else core

        def take_self(piece):
            if moved is not None:
                @pl.when(moved)
                def _():
                    if piece + AHEAD <= tail:
                        start_own(level, piece + AHEAD)
                    remote(level, 0, 1, 0, piece, 1 - core, mate).wait_recv()
                    hand_on(level, 1, piece)

        def take(slot, piece):
            remote(level, 0, slot, 0, piece, core, mate).wait_recv()

        def take_near(piece):
            take(2, piece)
            split(level, self_slot, piece, 1 - core, *((s1h, s1l) if piece < PER else (s2h, s2l)))
            split(level, 2, piece, core, *((n1h, n1l) if piece < PER else (n2h, n2l)))

        def take_far(piece):
            take(3, piece)
            split(level, 3, piece, core, *((f1h, f1l) if piece < PER else (f2h, f2l)))

        def first_term(r):
            rows = pl.ds(r * half, half)
            acc[rows, :] = dot3(s1h[rows, :], s1l[rows, :], f1h[...], f1l[...])

        def near_coupling(r):
            rows = pl.ds(r * half, half)
            store(xh.at[core], xl.at[core], rows, dot3(s2h[rows, :], s2l[rows, :], n1h[...], n1l[...]))

        def far_coupling(k):
            inner = pl.ds(k * half, half)
            for r in range(2):
                rows = pl.ds(r * half, half)
                value = dot3(s1h[rows, inner], s1l[rows, inner], f2h[inner, :], f2l[inner, :])
                if k == 0:
                    part[rows, :] = value
                else:
                    store(xh.at[1 - core], xl.at[1 - core], rows, part[rows, :] + value)

        def inverse():
            @pl.loop(0, 2)
            def _(r):
                store(eh, el, block(r), acc[block(r), :] + dot3(s2h[block(r), :], s2l[block(r), :], n2h[...], n2l[...]))

            @pl.loop(0, 2)
            def _(r):
                store(qh, ql, block(r), dot3(eh[block(r), :], el[block(r), :], eh[...], el[...]))

            @pl.loop(0, 2)
            def _(r):
                rows = lax.broadcasted_iota(jnp.int32, (half, order), 0) + r * half
                cols = lax.broadcasted_iota(jnp.int32, (half, order), 1)
                eye = jnp.where(rows == cols, 1.0, 0.0).astype(F32)
                value = dot3(eh[block(r), :], el[block(r), :], qh[...], ql[...])
                e = eh[block(r), :].astype(F32) + el[block(r), :].astype(F32)
                q = qh[block(r), :].astype(F32) + ql[block(r), :].astype(F32)
                store(yh, yl, block(r), eye + (e + (q + value)))

        def emit(position):
            which = (position + order_next) % 2

            @pl.loop(0, 2)
            def _(r):
                value = dot3(yh[block(r), :], yl[block(r), :], xh[which], xl[which])
                rows = pl.ds(pl.multiple_of(which * order + r * half, half), half)
                if level < LEVELS - 1:
                    bufs[level + 1, 0, rows, :] = -value
                else:
                    fin[rows, :] = value * (-factor)
                for t in range(PER // 2):
                    at = r * (PER // 2) + t
                    if level < LEVELS - 1:
                        send_own(level + 1, position * PER + at)
                    else:
                        out_rows = pl.ds(pl.multiple_of(at * size, size), size)

                        @pl.when(which == 0)
                        def _():
                            send_fin(at, out_upper, out_rows)

                        @pl.when(which == 1)
                        def _():
                            send_fin(PER + at, out_lower, out_rows)

        if level == 0:
            for piece in range(tail):
                take_near(piece)
            for r in range(2):
                near_coupling(r)
            for piece in range(PER):
                take_far(piece)
            for r in range(2):
                first_term(r)
            inverse()
            for piece in range(PER, tail - PER // 2):
                take_far(piece)
            far_coupling(0)
            for piece in range(tail - PER // 2, tail):
                take_far(piece)
        else:
            work = {
                PER + 1: functools.partial(first_term, 0),
                PER + 2: functools.partial(first_term, 1),
                PER + PER // 2 + 1: functools.partial(near_coupling, 0),
                PER + PER // 2 + 2: functools.partial(far_coupling, 0),
            }
            for step in range(tail + 1):
                take_self(step)
                if step >= 1:
                    take_near(step - 1)
                if step >= LAG:
                    take_far(step - LAG)
                if step in work:
                    work[step]()
            inverse()
            near_coupling(1)

        if level == LEVELS - 1:
            emit(0)
        else:
            @pl.when(order_next == core)
            def _():
                emit(0)

        if level:
            for piece in range(tail + 1 - LAG, tail):
                take_far(piece)
        far_coupling(1)
        if level < LEVELS - 1:
            @pl.when(order_next != core)
            def _():
                emit(0)

        emit(1)

        take(2, tail)
        take(3, tail)
        near_high, near_low = halves(bufs[level, 2, rows_of(tail, 0), :])
        far_high, far_low = halves(bufs[level, 3, rows_of(tail, 0), :])
        right = (bufs[level, self_slot, rows_of(tail, 0), :]
                 - dot3(near_high, near_low, s2h[...], s2l[...], True)
                 - dot3(far_high, far_low, s1h[...], s1l[...], True))
        right_high, right_low = halves(right)
        right = dot3(right_high, right_low, yh[...], yl[...], True)
        if level < LEVELS - 1:
            bufs[level + 1, 0, rows_of(tail, 0), :] = right
            send_own(level + 1, tail)
        else:
            fin[rows_of(tail, 0), :] = right
            send_fin(tail, out_rhs, pl.ds(0, columns))

    for level in range(LEVELS):
        for piece in range(tail + 1):
            if level:
                @pl.when(target[level] != me)
                def _():
                    remote(level, 0, 1, 0, piece, core, target[level]).wait_send()
            remote(level, 0, 2, 1, piece, core, mate).wait_send()
            remote(level, 0, 3, 2, piece, core, partner[level]).wait_send()

    ends = [(p, out_lower if p >= PER else out_upper, pl.ds((p % PER) * size, size)) for p in range(tail)]
    ends.append((tail, out_rhs, pl.ds(0, columns)))
    for piece, out, out_rows in ends:
        @pl.when(moves)
        def _():
            copy = fin_copy(piece, out, out_rows)
            copy.wait_send()
            copy.wait_recv()

        @pl.when(jnp.logical_not(moves))
        def _():
            fin_local(piece, out, out_rows).wait()


def settle(*refs):
    sources, results, held, in_sem, out_sem = refs[:3], refs[3:6], refs[6:9], refs[9], refs[10]
    quarters = []
    for part in range(4):
        for which in range(3):
            rows = held[which].shape[1] // 4
            at = pl.ds(part * rows, rows)
            load = pltpu.make_async_copy(sources[which].at[0, at], held[which].at[0, at], in_sem.at[which, part])
            keep = pltpu.make_async_copy(held[which].at[0, at], results[which].at[0, at], out_sem.at[which, part])
            load.start()
            quarters.append((load, keep))
    for load, keep in quarters:
        load.wait()
        keep.start()
    for _, keep in quarters:
        keep.wait()


def per_device(lower_block, upper_block, right_side):
    n = lax.axis_size("layer")
    order, columns = lower_block.shape[2], right_side.shape[1]
    rows = 2 * order + columns
    one = lambda: pltpu.VMEM((order, order), BF16)
    pieces = 2 * PER + 1
    reduced = pl.pallas_call(
        functools.partial(kernel, n, order, columns, 2.5**8 * math.sqrt(order)),
        out_shape=[jax.ShapeDtypeStruct(a.shape, F32) for a in (lower_block, upper_block, right_side)],
        in_specs=[pl.BlockSpec(memory_space=pl.ANY)] * 3,
        out_specs=[pl.BlockSpec(memory_space=pl.ANY)] * 3,
        scratch_shapes=[
            pltpu.VMEM((LEVELS, 4, rows, order), F32),
            pltpu.VMEM((rows, order), F32),
            pltpu.VMEM((order, order), F32),
            pltpu.VMEM((order, order), F32),
            pltpu.VMEM((2, order, order), BF16),
            pltpu.VMEM((2, order, order), BF16),
            *[one() for _ in range(18)],
            pltpu.SemaphoreType.DMA((pieces,)),
            pltpu.SemaphoreType.DMA((LEVELS, 3, pieces)),
            pltpu.SemaphoreType.DMA((LEVELS, 3, pieces)),
            pltpu.SemaphoreType.DMA((pieces,)),
            pltpu.SemaphoreType.DMA((pieces,)),
        ],
        compiler_params=pltpu.CompilerParams(
            collective_id=0, has_side_effects=True, vmem_limit_bytes=60 * 1024 * 1024
        ),
    )(lower_block, upper_block, right_side)
    return pl.pallas_call(
        settle,
        out_shape=[jax.ShapeDtypeStruct(a.shape, F32) for a in reduced],
        in_specs=[pl.BlockSpec(memory_space=pl.ANY)] * 3,
        out_specs=[pl.BlockSpec(memory_space=pl.ANY)] * 3,
        scratch_shapes=[
            *[pltpu.VMEM(a.shape, F32) for a in reduced],
            pltpu.SemaphoreType.DMA((3, 4)),
            pltpu.SemaphoreType.DMA((3, 4)),
        ],
    )(*reduced)


def solution(mesh):
    placed = (P("layer", None, None), P("layer", None, None), P("layer", None, None))
    return jax.shard_map(
        per_device,
        mesh=mesh,
        in_specs=placed,
        out_specs=placed,
        check_vma=False,
    )
```

```python
import functools
import math

import jax
import jax.numpy as jnp
from jax import lax
from jax.experimental import pallas as pl
from jax.experimental.pallas import tpu as pltpu
from jax.sharding import PartitionSpec as P

LEVELS = 3
CHAINS = 8
PER = 8
AHEAD = 2
LAG = 3
F32, BF16 = jnp.float32, jnp.bfloat16
MESH = pl.DeviceIdType.MESH


def halves(value):
    high = value.astype(BF16)
    return high, (value - high.astype(F32)).astype(BF16)


def dot3(a_high, a_low, b_high, b_low, transposed=False):
    dims = (((1,), (1 if transposed else 0,)), ((), ()))
    dot = lambda a, b: lax.dot_general(a, b, dims, preferred_element_type=F32)
    return dot(a_high, b_high) + (dot(a_high, b_low) + dot(a_low, b_high))


def placements(n):
    planes = n // CHAINS
    quarter = planes // 4

    def parts(layer):
        j, r = layer // CHAINS, layer % CHAINS
        return j // (2 * quarter), (j // 2) % quarter, j % 2, r // 4, (r // 2) % 2, r % 2

    def join(b4, mid, b3, b2, b1, b0):
        return CHAINS * (b4 * 2 * quarter + mid * 2 + b3) + 4 * b2 + 2 * b1 + b0

    def middle(layer):
        b4, mid, b3, b2, b1, b0 = parts(layer)
        return 8 * ((b0 * 2 + b4) * quarter + mid) + 4 * b2 + 2 * ((b4 + b3) % 2) + b1

    def middle_layer(dev):
        z, y, x, core = dev // 8, (dev // 4) % 2, (dev // 2) % 2, dev % 2
        b0, b4, mid = z // (2 * quarter), (z // quarter) % 2, z % quarter
        return join(b4, mid, (x + b4) % 2, y, core, b0)

    def last(layer):
        b4, mid, b3, b2, b1, b0 = parts(layer)
        return 8 * ((b0 * 2 + b4) * quarter + mid) + 4 * ((b1 + b0) % 2) + 2 * ((b4 + b3) % 2) + b2

    def last_layer(dev):
        z, y, x, core = dev // 8, (dev // 4) % 2, (dev // 2) % 2, dev % 2
        b0, b4, mid = z // (2 * quarter), (z // quarter) % 2, z % quarter
        return join(b4, mid, (x + b4) % 2, core, (y + b0) % 2, b0)

    def regrouped(layer):
        return (layer % CHAINS) * planes + layer // CHAINS

    def regrouped_layer(dev):
        return (dev % planes) * CHAINS + dev // planes

    same = lambda at: at
    return (same, middle, last, regrouped), (same, middle_layer, last_layer, regrouped_layer)


def kernel(n, order, columns, factor, lower_ref, upper_ref, rhs_ref, out_lower, out_upper, out_rhs,
           bufs, fin, acc, part, xh, xl, s1h, s1l, s2h, s2l, n1h, n1l, n2h, n2l, f1h, f1l, f2h, f2l,
           eh, el, qh, ql, yh, yl,
           load_sem, send_sem, recv_sem, fin_send, fin_recv):
    me = lax.axis_index("layer")
    core = me % 2
    mate = me + 1 - 2 * core
    half = order // 2
    size = order // PER
    tail = 2 * PER
    device_of, layer_of = placements(n)

    partner, target, source = [], [None], [None]
    for level in range(LEVELS):
        stride = 1 << level
        mine = layer_of[level](me)
        partner.append(device_of[level]((mine + stride * (2 * core - 1) + n) % n))
        target.append(device_of[level + 1](mine))
        source.append(device_of[level](layer_of[level + 1](me)))
    goes_to, comes_from = target[LEVELS], source[LEVELS]
    moves = goes_to != me

    def rows_of(piece, first):
        if isinstance(piece, int) and piece == tail:
            return pl.ds(2 * order, columns)
        which = (piece // PER + first) % 2
        return pl.ds(pl.multiple_of(which * order + (piece % PER) * size, size), size)

    def remote(level, from_slot, to_slot, flow, piece, first, dev):
        return pltpu.make_async_remote_copy(
            src_ref=bufs.at[level, from_slot, rows_of(piece, first)],
            dst_ref=bufs.at[level, to_slot, rows_of(piece, first)],
            send_sem=send_sem.at[level, flow, piece],
            recv_sem=recv_sem.at[level, to_slot - 1, piece],
            device_id=(dev,),
            device_id_type=MESH,
        )

    def hand_on(level, slot, piece):
        remote(level, slot, 3, 2, piece, 1 - core, partner[level]).start()
        remote(level, slot, 2, 1, piece, 1 - core, mate).start()

    def start_own(level, piece):
        remote(level, 0, 1, 0, piece, 1 - target[level] % 2, target[level]).start()

    def send_own(level, piece):
        @pl.when((target[level] != me) & (piece < AHEAD))
        def _():
            start_own(level, piece)

        @pl.when(target[level] == me)
        def _():
            hand_on(level, 0, piece)

    barrier = pltpu.get_barrier_semaphore()

    def greet(dev):
        pl.semaphore_signal(barrier, inc=1, device_id=(dev,), device_id_type=MESH)

    loads = []
    for index, (ref, start, count) in enumerate(((upper_ref, 0, order), (lower_ref, order, order), (rhs_ref, 2 * order, columns))):
        copy = pltpu.make_async_copy(ref.at[0], bufs.at[0, 0, pl.ds(start, count)], load_sem.at[index])
        copy.start()
        loads.append(copy)

    greet(mate)
    expected = jnp.int32(1 + LEVELS)
    for level in range(LEVELS):
        greet(partner[level])
    for level in range(1, LEVELS + 1):
        @pl.when(source[level] != me)
        def _():
            greet(source[level])

        expected += (target[level] != me).astype(jnp.int32)
    pl.semaphore_wait(barrier, expected)

    for copy in loads:
        copy.wait()
    for piece in range(tail + 1):
        hand_on(0, 0, piece)

    def block(r):
        return pl.ds(pl.multiple_of(r * half, half), half)

    def split(level, slot, piece, first, high_ref, low_ref):
        high, low = halves(bufs[level, slot, rows_of(piece, first), :])
        rows = pl.ds((piece % PER) * size, size)
        high_ref[rows, :] = high
        low_ref[rows, :] = low

    def store(high_ref, low_ref, rows, value):
        high, low = halves(value)
        high_ref[rows, :] = high
        low_ref[rows, :] = low


    def fin_copy(piece, out, out_rows):
        return pltpu.make_async_remote_copy(
            src_ref=fin.at[rows_of(piece, 0)], dst_ref=out.at[0, out_rows],
            send_sem=fin_send.at[piece], recv_sem=fin_recv.at[piece],
            device_id=(goes_to,), device_id_type=MESH)

    def fin_local(piece, out, out_rows):
        return pltpu.make_async_copy(fin.at[rows_of(piece, 0)], out.at[0, out_rows], load_sem.at[piece])

    def send_fin(piece, out, out_rows):
        @pl.when(moves)
        def _():
            fin_copy(piece, out, out_rows).start()

        @pl.when(jnp.logical_not(moves))
        def _():
            fin_local(piece, out, out_rows).start()

    for level in range(LEVELS):
        if level:
            moved = source[level] != me
            self_slot = jnp.where(moved, 1, 0)
        else:
            moved, self_slot = None, 0
        order_next = 1 - target[level + 1] % 2 if level < LEVELS - 1 else core

        def take_self(piece):
            if moved is not None:
                @pl.when(moved)
                def _():
                    if piece + AHEAD <= tail:
                        start_own(level, piece + AHEAD)
                    remote(level, 0, 1, 0, piece, 1 - core, mate).wait_recv()
                    hand_on(level, 1, piece)

        def take(slot, piece):
            remote(level, 0, slot, 0, piece, core, mate).wait_recv()

        def take_near(piece):
            take(2, piece)
            split(level, self_slot, piece, 1 - core, *((s1h, s1l) if piece < PER else (s2h, s2l)))
            split(level, 2, piece, core, *((n1h, n1l) if piece < PER else (n2h, n2l)))

        def take_far(piece):
            take(3, piece)
            split(level, 3, piece, core, *((f1h, f1l) if piece < PER else (f2h, f2l)))

        def first_term(r):
            rows = pl.ds(r * half, half)
            acc[rows, :] = dot3(s1h[rows, :], s1l[rows, :], f1h[...], f1l[...])

        def near_coupling(r):
            rows = pl.ds(r * half, half)
            store(xh.at[core], xl.at[core], rows, dot3(s2h[rows, :], s2l[rows, :], n1h[...], n1l[...]))

        def far_coupling(k):
            inner = pl.ds(k * half, half)
            for r in range(2):
                rows = pl.ds(r * half, half)
                value = dot3(s1h[rows, inner], s1l[rows, inner], f2h[inner, :], f2l[inner, :])
                if k == 0:
                    part[rows, :] = value
                else:
                    store(xh.at[1 - core], xl.at[1 - core], rows, part[rows, :] + value)

        def inverse():
            @pl.loop(0, 2)
            def _(r):
                store(eh, el, block(r), acc[block(r), :] + dot3(s2h[block(r), :], s2l[block(r), :], n2h[...], n2l[...]))

            @pl.loop(0, 2)
            def _(r):
                store(qh, ql, block(r), dot3(eh[block(r), :], el[block(r), :], eh[...], el[...]))

            @pl.loop(0, 2)
            def _(r):
                rows = lax.broadcasted_iota(jnp.int32, (half, order), 0) + r * half
                cols = lax.broadcasted_iota(jnp.int32, (half, order), 1)
                eye = jnp.where(rows == cols, 1.0, 0.0).astype(F32)
                value = dot3(eh[block(r), :], el[block(r), :], qh[...], ql[...])
                e = eh[block(r), :].astype(F32) + el[block(r), :].astype(F32)
                q = qh[block(r), :].astype(F32) + ql[block(r), :].astype(F32)
                store(yh, yl, block(r), eye + (e + (q + value)))

        def emit(position):
            which = (position + order_next) % 2

            @pl.loop(0, 2)
            def _(r):
                value = dot3(yh[block(r), :], yl[block(r), :], xh[which], xl[which])
                rows = pl.ds(pl.multiple_of(which * order + r * half, half), half)
                if level < LEVELS - 1:
                    bufs[level + 1, 0, rows, :] = -value
                else:
                    fin[rows, :] = value * (-factor)
                for t in range(PER // 2):
                    at = r * (PER // 2) + t
                    if level < LEVELS - 1:
                        send_own(level + 1, position * PER + at)
                    else:
                        out_rows = pl.ds(pl.multiple_of(at * size, size), size)

                        @pl.when(which == 0)
                        def _():
                            send_fin(at, out_upper, out_rows)

                        @pl.when(which == 1)
                        def _():
                            send_fin(PER + at, out_lower, out_rows)

        if level == 0:
            for piece in range(tail):
                take_near(piece)
            for r in range(2):
                near_coupling(r)
            for piece in range(PER):
                take_far(piece)
            for r in range(2):
                first_term(r)
            inverse()
            for piece in range(PER, tail - PER // 2):
                take_far(piece)
            far_coupling(0)
            for piece in range(tail - PER // 2, tail):
                take_far(piece)
        else:
            work = {
                PER + LAG - 1: functools.partial(first_term, 0),
                PER + LAG: functools.partial(first_term, 1),
                PER + PER // 2 + LAG - 1: functools.partial(near_coupling, 0),
                PER + PER // 2 + LAG: functools.partial(far_coupling, 0),
            }
            for step in range(tail + 1):
                take_self(step)
                if step >= 1:
                    take_near(step - 1)
                if step >= LAG:
                    take_far(step - LAG)
                if step in work:
                    work[step]()
            inverse()
            near_coupling(1)

        if level == LEVELS - 1:
            emit(0)
        else:
            @pl.when(order_next == core)
            def _():
                emit(0)

        if level:
            for piece in range(tail + 1 - LAG, tail):
                take_far(piece)
        far_coupling(1)
        if level < LEVELS - 1:
            @pl.when(order_next != core)
            def _():
                emit(0)

        emit(1)

        take(2, tail)
        take(3, tail)
        near_high, near_low = halves(bufs[level, 2, rows_of(tail, 0), :])
        far_high, far_low = halves(bufs[level, 3, rows_of(tail, 0), :])
        right = (bufs[level, self_slot, rows_of(tail, 0), :]
                 - dot3(near_high, near_low, s2h[...], s2l[...], True)
                 - dot3(far_high, far_low, s1h[...], s1l[...], True))
        right_high, right_low = halves(right)
        right = dot3(right_high, right_low, yh[...], yl[...], True)
        if level < LEVELS - 1:
            bufs[level + 1, 0, rows_of(tail, 0), :] = right
            send_own(level + 1, tail)
        else:
            fin[rows_of(tail, 0), :] = right
            send_fin(tail, out_rhs, pl.ds(0, columns))

    for level in range(LEVELS):
        for piece in range(tail + 1):
            if level:
                @pl.when(target[level] != me)
                def _():
                    remote(level, 0, 1, 0, piece, core, target[level]).wait_send()
            remote(level, 0, 2, 1, piece, core, mate).wait_send()
            remote(level, 0, 3, 2, piece, core, partner[level]).wait_send()

    ends = [(p, out_lower if p >= PER else out_upper, pl.ds((p % PER) * size, size)) for p in range(tail)]
    ends.append((tail, out_rhs, pl.ds(0, columns)))
    for piece, out, out_rows in ends:
        @pl.when(moves)
        def _():
            copy = fin_copy(piece, out, out_rows)
            copy.wait_send()
            copy.wait_recv()

        @pl.when(jnp.logical_not(moves))
        def _():
            fin_local(piece, out, out_rows).wait()


def settle(*refs):
    sources, results, held, in_sem, out_sem = refs[:3], refs[3:6], refs[6:9], refs[9], refs[10]
    quarters = []
    for part in range(4):
        for which in range(3):
            rows = held[which].shape[1] // 4
            at = pl.ds(part * rows, rows)
            load = pltpu.make_async_copy(sources[which].at[0, at], held[which].at[0, at], in_sem.at[which, part])
            keep = pltpu.make_async_copy(held[which].at[0, at], results[which].at[0, at], out_sem.at[which, part])
            load.start()
            quarters.append((load, keep))
    for load, keep in quarters:
        load.wait()
        keep.start()
    for _, keep in quarters:
        keep.wait()


def per_device(lower_block, upper_block, right_side):
    n = lax.axis_size("layer")
    order, columns = lower_block.shape[2], right_side.shape[1]
    rows = 2 * order + columns
    one = lambda: pltpu.VMEM((order, order), BF16)
    pieces = 2 * PER + 1
    reduced = pl.pallas_call(
        functools.partial(kernel, n, order, columns, 2.5**8 * math.sqrt(order)),
        out_shape=[jax.ShapeDtypeStruct(a.shape, F32) for a in (lower_block, upper_block, right_side)],
        in_specs=[pl.BlockSpec(memory_space=pl.ANY)] * 3,
        out_specs=[pl.BlockSpec(memory_space=pl.ANY)] * 3,
        scratch_shapes=[
            pltpu.VMEM((LEVELS, 4, rows, order), F32),
            pltpu.VMEM((rows, order), F32),
            pltpu.VMEM((order, order), F32),
            pltpu.VMEM((order, order), F32),
            pltpu.VMEM((2, order, order), BF16),
            pltpu.VMEM((2, order, order), BF16),
            *[one() for _ in range(18)],
            pltpu.SemaphoreType.DMA((pieces,)),
            pltpu.SemaphoreType.DMA((LEVELS, 3, pieces)),
            pltpu.SemaphoreType.DMA((LEVELS, 3, pieces)),
            pltpu.SemaphoreType.DMA((pieces,)),
            pltpu.SemaphoreType.DMA((pieces,)),
        ],
        compiler_params=pltpu.CompilerParams(
            collective_id=0, has_side_effects=True, vmem_limit_bytes=60 * 1024 * 1024
        ),
    )(lower_block, upper_block, right_side)
    return pl.pallas_call(
        settle,
        out_shape=[jax.ShapeDtypeStruct(a.shape, F32) for a in reduced],
        in_specs=[pl.BlockSpec(memory_space=pl.ANY)] * 3,
        out_specs=[pl.BlockSpec(memory_space=pl.ANY)] * 3,
        scratch_shapes=[
            *[pltpu.VMEM(a.shape, F32) for a in reduced],
            pltpu.SemaphoreType.DMA((3, 4)),
            pltpu.SemaphoreType.DMA((3, 4)),
        ],
    )(*reduced)


def solution(mesh):
    placed = (P("layer", None, None), P("layer", None, None), P("layer", None, None))
    return jax.shard_map(
        per_device,
        mesh=mesh,
        in_specs=placed,
        out_specs=placed,
        check_vma=False,
    )
```

```python
import functools
import math

import jax
import jax.numpy as jnp
from jax import lax
from jax.experimental import pallas as pl
from jax.experimental.pallas import tpu as pltpu
from jax.sharding import PartitionSpec as P

LEVELS = 3
CHAINS = 8
PER = 8
AHEAD = 2
LAG = 3
F32, BF16 = jnp.float32, jnp.bfloat16
MESH = pl.DeviceIdType.MESH


def halves(value):
    high = value.astype(BF16)
    return high, (value - high.astype(F32)).astype(BF16)


def dot3(a_high, a_low, b_high, b_low, transposed=False):
    dims = (((1,), (1 if transposed else 0,)), ((), ()))
    dot = lambda a, b: lax.dot_general(a, b, dims, preferred_element_type=F32)
    return dot(a_high, b_high) + (dot(a_high, b_low) + dot(a_low, b_high))


def placements(n):
    planes = n // CHAINS
    quarter = planes // 4

    def parts(layer):
        j, r = layer // CHAINS, layer % CHAINS
        return j // (2 * quarter), (j // 2) % quarter, j % 2, r // 4, (r // 2) % 2, r % 2

    def join(b4, mid, b3, b2, b1, b0):
        return CHAINS * (b4 * 2 * quarter + mid * 2 + b3) + 4 * b2 + 2 * b1 + b0

    def middle(layer):
        b4, mid, b3, b2, b1, b0 = parts(layer)
        return 8 * ((b0 * 2 + b4) * quarter + mid) + 4 * b2 + 2 * ((b4 + b3) % 2) + b1

    def middle_layer(dev):
        z, y, x, core = dev // 8, (dev // 4) % 2, (dev // 2) % 2, dev % 2
        b0, b4, mid = z // (2 * quarter), (z // quarter) % 2, z % quarter
        return join(b4, mid, (x + b4) % 2, y, core, b0)

    def last(layer):
        b4, mid, b3, b2, b1, b0 = parts(layer)
        return 8 * ((b0 * 2 + b4) * quarter + mid) + 4 * ((b1 + b0) % 2) + 2 * ((b4 + b3) % 2) + b2

    def last_layer(dev):
        z, y, x, core = dev // 8, (dev // 4) % 2, (dev // 2) % 2, dev % 2
        b0, b4, mid = z // (2 * quarter), (z // quarter) % 2, z % quarter
        return join(b4, mid, (x + b4) % 2, core, (y + b0) % 2, b0)

    def regrouped(layer):
        return (layer % CHAINS) * planes + layer // CHAINS

    def regrouped_layer(dev):
        return (dev % planes) * CHAINS + dev // planes

    same = lambda at: at
    return (same, middle, last, regrouped), (same, middle_layer, last_layer, regrouped_layer)


def kernel(n, order, columns, factor, lower_ref, upper_ref, rhs_ref, out_lower, out_upper, out_rhs,
           bufs, fin, acc, part, xh, xl, s1h, s1l, s2h, s2l, n1h, n1l, n2h, n2l, f1h, f1l, f2h, f2l,
           eh, el, qh, ql, yh, yl,
           load_sem, send_sem, recv_sem, fin_send, fin_recv):
    me = lax.axis_index("layer")
    core = me % 2
    mate = me + 1 - 2 * core
    half = order // 2
    size = order // PER
    tail = 2 * PER
    device_of, layer_of = placements(n)

    partner, target, source = [], [None], [None]
    for level in range(LEVELS):
        stride = 1 << level
        mine = layer_of[level](me)
        partner.append(device_of[level]((mine + stride * (2 * core - 1) + n) % n))
        target.append(device_of[level + 1](mine))
        source.append(device_of[level](layer_of[level + 1](me)))
    goes_to, comes_from = target[LEVELS], source[LEVELS]
    moves = goes_to != me

    def rows_of(piece, first):
        if isinstance(piece, int) and piece == tail:
            return pl.ds(2 * order, columns)
        which = (piece // PER + first) % 2
        return pl.ds(pl.multiple_of(which * order + (piece % PER) * size, size), size)

    def remote(level, from_slot, to_slot, flow, piece, first, dev):
        return pltpu.make_async_remote_copy(
            src_ref=bufs.at[level, from_slot, rows_of(piece, first)],
            dst_ref=bufs.at[level, to_slot, rows_of(piece, first)],
            send_sem=send_sem.at[level, flow, piece],
            recv_sem=recv_sem.at[level, to_slot - 1, piece],
            device_id=(dev,),
            device_id_type=MESH,
        )

    def hand_on(level, slot, piece):
        remote(level, slot, 3, 2, piece, 1 - core, partner[level]).start()
        remote(level, slot, 2, 1, piece, 1 - core, mate).start()

    def start_own(level, piece):
        remote(level, 0, 1, 0, piece, 1 - target[level] % 2, target[level]).start()

    def send_own(level, piece):
        @pl.when((target[level] != me) & (piece < AHEAD))
        def _():
            start_own(level, piece)

        @pl.when(target[level] == me)
        def _():
            hand_on(level, 0, piece)

    barrier = pltpu.get_barrier_semaphore()

    def greet(dev):
        pl.semaphore_signal(barrier, inc=1, device_id=(dev,), device_id_type=MESH)

    loads = []
    for index, (ref, start, count) in enumerate(((upper_ref, 0, order), (lower_ref, order, order), (rhs_ref, 2 * order, columns))):
        copy = pltpu.make_async_copy(ref.at[0], bufs.at[0, 0, pl.ds(start, count)], load_sem.at[index])
        copy.start()
        loads.append(copy)

    greet(mate)
    expected = jnp.int32(1 + LEVELS)
    for level in range(LEVELS):
        greet(partner[level])
    for level in range(1, LEVELS + 1):
        @pl.when(source[level] != me)
        def _():
            greet(source[level])

        expected += (target[level] != me).astype(jnp.int32)
    pl.semaphore_wait(barrier, expected)

    for copy in loads:
        copy.wait()
    for piece in range(tail + 1):
        hand_on(0, 0, piece)

    def block(r):
        return pl.ds(pl.multiple_of(r * half, half), half)

    def split(level, slot, piece, first, high_ref, low_ref):
        high, low = halves(bufs[level, slot, rows_of(piece, first), :])
        rows = pl.ds((piece % PER) * size, size)
        high_ref[rows, :] = high
        low_ref[rows, :] = low

    def store(high_ref, low_ref, rows, value):
        high, low = halves(value)
        high_ref[rows, :] = high
        low_ref[rows, :] = low


    def fin_copy(piece, out, out_rows):
        return pltpu.make_async_remote_copy(
            src_ref=fin.at[rows_of(piece, 0)], dst_ref=out.at[0, out_rows],
            send_sem=fin_send.at[piece], recv_sem=fin_recv.at[piece],
            device_id=(goes_to,), device_id_type=MESH)

    def fin_local(piece, out, out_rows):
        return pltpu.make_async_copy(fin.at[rows_of(piece, 0)], out.at[0, out_rows], load_sem.at[piece])

    def send_fin(piece, out, out_rows):
        @pl.when(moves)
        def _():
            fin_copy(piece, out, out_rows).start()

        @pl.when(jnp.logical_not(moves))
        def _():
            fin_local(piece, out, out_rows).start()

    for level in range(LEVELS):
        if level:
            moved = source[level] != me
            self_slot = jnp.where(moved, 1, 0)
        else:
            moved, self_slot = None, 0
        order_next = 1 - target[level + 1] % 2 if level < LEVELS - 1 else core

        def take_self(piece):
            if moved is not None:
                @pl.when(moved)
                def _():
                    if piece + AHEAD <= tail:
                        start_own(level, piece + AHEAD)
                    remote(level, 0, 1, 0, piece, 1 - core, mate).wait_recv()
                    hand_on(level, 1, piece)

        def take(slot, piece):
            remote(level, 0, slot, 0, piece, core, mate).wait_recv()

        def take_near(piece):
            take(2, piece)
            split(level, self_slot, piece, 1 - core, *((s1h, s1l) if piece < PER else (s2h, s2l)))
            split(level, 2, piece, core, *((n1h, n1l) if piece < PER else (n2h, n2l)))

        def take_far(piece):
            take(3, piece)
            split(level, 3, piece, core, *((f1h, f1l) if piece < PER else (f2h, f2l)))

        def first_term(r):
            rows = pl.ds(r * half, half)
            acc[rows, :] = dot3(s1h[rows, :], s1l[rows, :], f1h[...], f1l[...])

        def near_coupling(r):
            rows = pl.ds(r * half, half)
            store(xh.at[core], xl.at[core], rows, dot3(s2h[rows, :], s2l[rows, :], n1h[...], n1l[...]))

        def far_coupling(k):
            inner = pl.ds(k * half, half)
            value = dot3(s1h[:, inner], s1l[:, inner], f2h[inner, :], f2l[inner, :])
            if k == 0:
                part[...] = value
            else:
                store(xh.at[1 - core], xl.at[1 - core], pl.ds(0, order), part[...] + value)

        def inverse():
            every = pl.ds(0, order)
            store(eh, el, every, acc[...] + dot3(s2h[...], s2l[...], n2h[...], n2l[...]))
            store(qh, ql, every, dot3(eh[...], el[...], eh[...], el[...]))
            rows = lax.broadcasted_iota(jnp.int32, (order, order), 0)
            cols = lax.broadcasted_iota(jnp.int32, (order, order), 1)
            eye = jnp.where(rows == cols, 1.0, 0.0).astype(F32)
            value = dot3(eh[...], el[...], qh[...], ql[...])
            e = eh[...].astype(F32) + el[...].astype(F32)
            q = qh[...].astype(F32) + ql[...].astype(F32)
            store(yh, yl, every, eye + (e + (q + value)))

        def emit(position):
            which = (position + order_next) % 2

            @pl.loop(0, 2)
            def _(r):
                value = dot3(yh[block(r), :], yl[block(r), :], xh[which], xl[which])
                rows = pl.ds(pl.multiple_of(which * order + r * half, half), half)
                if level < LEVELS - 1:
                    bufs[level + 1, 0, rows, :] = -value
                else:
                    fin[rows, :] = value * (-factor)
                for t in range(PER // 2):
                    at = r * (PER // 2) + t
                    if level < LEVELS - 1:
                        send_own(level + 1, position * PER + at)
                    else:
                        out_rows = pl.ds(pl.multiple_of(at * size, size), size)

                        @pl.when(which == 0)
                        def _():
                            send_fin(at, out_upper, out_rows)

                        @pl.when(which == 1)
                        def _():
                            send_fin(PER + at, out_lower, out_rows)

        if level == 0:
            for piece in range(tail):
                take_near(piece)
            near_coupling(0)
            near_coupling(1)
            for piece in range(PER):
                take_far(piece)
            for r in range(2):
                first_term(r)
            inverse()
            for piece in range(PER, tail - PER // 2):
                take_far(piece)
            far_coupling(0)
            for piece in range(tail - PER // 2, tail):
                take_far(piece)
        else:
            work = {
                PER + LAG - 1: functools.partial(first_term, 0),
                PER + LAG: functools.partial(first_term, 1),
                PER + PER // 2 + LAG - 1: functools.partial(near_coupling, 0),
                PER + PER // 2 + LAG: functools.partial(far_coupling, 0),
            }
            for step in range(tail + 1):
                take_self(step)
                if step >= 1:
                    take_near(step - 1)
                if step >= LAG:
                    take_far(step - LAG)
                if step in work:
                    work[step]()
            inverse()
            near_coupling(1)

        if level == LEVELS - 1:
            emit(0)
        else:
            @pl.when(order_next == core)
            def _():
                emit(0)

        if level:
            for piece in range(tail + 1 - LAG, tail):
                take_far(piece)
        far_coupling(1)
        if level < LEVELS - 1:
            @pl.when(order_next != core)
            def _():
                emit(0)

        emit(1)

        take(2, tail)
        take(3, tail)
        near_high, near_low = halves(bufs[level, 2, rows_of(tail, 0), :])
        far_high, far_low = halves(bufs[level, 3, rows_of(tail, 0), :])
        right = (bufs[level, self_slot, rows_of(tail, 0), :]
                 - dot3(near_high, near_low, s2h[...], s2l[...], True)
                 - dot3(far_high, far_low, s1h[...], s1l[...], True))
        right_high, right_low = halves(right)
        right = dot3(right_high, right_low, yh[...], yl[...], True)
        if level < LEVELS - 1:
            bufs[level + 1, 0, rows_of(tail, 0), :] = right
            send_own(level + 1, tail)
        else:
            fin[rows_of(tail, 0), :] = right
            send_fin(tail, out_rhs, pl.ds(0, columns))

    for level in range(LEVELS):
        for piece in range(tail + 1):
            if level:
                @pl.when(target[level] != me)
                def _():
                    remote(level, 0, 1, 0, piece, core, target[level]).wait_send()
            remote(level, 0, 2, 1, piece, core, mate).wait_send()
            remote(level, 0, 3, 2, piece, core, partner[level]).wait_send()

    ends = [(p, out_lower if p >= PER else out_upper, pl.ds((p % PER) * size, size)) for p in range(tail)]
    ends.append((tail, out_rhs, pl.ds(0, columns)))
    for piece, out, out_rows in ends:
        @pl.when(moves)
        def _():
            copy = fin_copy(piece, out, out_rows)
            copy.wait_send()
            copy.wait_recv()

        @pl.when(jnp.logical_not(moves))
        def _():
            fin_local(piece, out, out_rows).wait()


def settle(*refs):
    sources, results, held, in_sem, out_sem = refs[:3], refs[3:6], refs[6:9], refs[9], refs[10]
    quarters = []
    for part in range(4):
        for which in range(3):
            rows = held[which].shape[1] // 4
            at = pl.ds(part * rows, rows)
            load = pltpu.make_async_copy(sources[which].at[0, at], held[which].at[0, at], in_sem.at[which, part])
            keep = pltpu.make_async_copy(held[which].at[0, at], results[which].at[0, at], out_sem.at[which, part])
            load.start()
            quarters.append((load, keep))
    for load, keep in quarters:
        load.wait()
        keep.start()
    for _, keep in quarters:
        keep.wait()


def per_device(lower_block, upper_block, right_side):
    n = lax.axis_size("layer")
    order, columns = lower_block.shape[2], right_side.shape[1]
    rows = 2 * order + columns
    one = lambda: pltpu.VMEM((order, order), BF16)
    pieces = 2 * PER + 1
    reduced = pl.pallas_call(
        functools.partial(kernel, n, order, columns, 2.5**8 * math.sqrt(order)),
        out_shape=[jax.ShapeDtypeStruct(a.shape, F32) for a in (lower_block, upper_block, right_side)],
        in_specs=[pl.BlockSpec(memory_space=pl.ANY)] * 3,
        out_specs=[pl.BlockSpec(memory_space=pl.ANY)] * 3,
        scratch_shapes=[
            pltpu.VMEM((LEVELS, 4, rows, order), F32),
            pltpu.VMEM((rows, order), F32),
            pltpu.VMEM((order, order), F32),
            pltpu.VMEM((order, order), F32),
            pltpu.VMEM((2, order, order), BF16),
            pltpu.VMEM((2, order, order), BF16),
            *[one() for _ in range(18)],
            pltpu.SemaphoreType.DMA((pieces,)),
            pltpu.SemaphoreType.DMA((LEVELS, 3, pieces)),
            pltpu.SemaphoreType.DMA((LEVELS, 3, pieces)),
            pltpu.SemaphoreType.DMA((pieces,)),
            pltpu.SemaphoreType.DMA((pieces,)),
        ],
        compiler_params=pltpu.CompilerParams(
            collective_id=0, has_side_effects=True, vmem_limit_bytes=60 * 1024 * 1024
        ),
    )(lower_block, upper_block, right_side)
    return pl.pallas_call(
        settle,
        out_shape=[jax.ShapeDtypeStruct(a.shape, F32) for a in reduced],
        in_specs=[pl.BlockSpec(memory_space=pl.ANY)] * 3,
        out_specs=[pl.BlockSpec(memory_space=pl.ANY)] * 3,
        scratch_shapes=[
            *[pltpu.VMEM(a.shape, F32) for a in reduced],
            pltpu.SemaphoreType.DMA((3, 4)),
            pltpu.SemaphoreType.DMA((3, 4)),
        ],
    )(*reduced)


def solution(mesh):
    placed = (P("layer", None, None), P("layer", None, None), P("layer", None, None))
    return jax.shard_map(
        per_device,
        mesh=mesh,
        in_specs=placed,
        out_specs=placed,
        check_vma=False,
    )
```

```python
import functools
import math

import jax
import jax.numpy as jnp
from jax import lax
from jax.experimental import pallas as pl
from jax.experimental.pallas import tpu as pltpu
from jax.sharding import PartitionSpec as P

LEVELS = 3
CHAINS = 8
PER = 8
AHEAD = 2
LAG = 3
F32, BF16 = jnp.float32, jnp.bfloat16
MESH = pl.DeviceIdType.MESH


def halves(value):
    high = value.astype(BF16)
    return high, (value - high.astype(F32)).astype(BF16)


def dot3(a_high, a_low, b_high, b_low, transposed=False):
    dims = (((1,), (1 if transposed else 0,)), ((), ()))
    dot = lambda a, b: lax.dot_general(a, b, dims, preferred_element_type=F32)
    return dot(a_high, b_high) + (dot(a_high, b_low) + dot(a_low, b_high))


def placements(n):
    planes = n // CHAINS
    quarter = planes // 4

    def parts(layer):
        j, r = layer // CHAINS, layer % CHAINS
        return j // (2 * quarter), (j // 2) % quarter, j % 2, r // 4, (r // 2) % 2, r % 2

    def join(b4, mid, b3, b2, b1, b0):
        return CHAINS * (b4 * 2 * quarter + mid * 2 + b3) + 4 * b2 + 2 * b1 + b0

    def middle(layer):
        b4, mid, b3, b2, b1, b0 = parts(layer)
        return 8 * ((b0 * 2 + b4) * quarter + mid) + 4 * b2 + 2 * ((b4 + b3) % 2) + b1

    def middle_layer(dev):
        z, y, x, core = dev // 8, (dev // 4) % 2, (dev // 2) % 2, dev % 2
        b0, b4, mid = z // (2 * quarter), (z // quarter) % 2, z % quarter
        return join(b4, mid, (x + b4) % 2, y, core, b0)

    def last(layer):
        b4, mid, b3, b2, b1, b0 = parts(layer)
        return 8 * ((b0 * 2 + b4) * quarter + mid) + 4 * ((b1 + b0) % 2) + 2 * ((b4 + b3) % 2) + b2

    def last_layer(dev):
        z, y, x, core = dev // 8, (dev // 4) % 2, (dev // 2) % 2, dev % 2
        b0, b4, mid = z // (2 * quarter), (z // quarter) % 2, z % quarter
        return join(b4, mid, (x + b4) % 2, core, (y + b0) % 2, b0)

    def regrouped(layer):
        return (layer % CHAINS) * planes + layer // CHAINS

    def regrouped_layer(dev):
        return (dev % planes) * CHAINS + dev // planes

    same = lambda at: at
    return (same, middle, last, regrouped), (same, middle_layer, last_layer, regrouped_layer)


def kernel(n, order, columns, factor, lower_ref, upper_ref, rhs_ref, out_lower, out_upper, out_rhs,
           bufs, fin, acc, part, xh, xl, s1h, s1l, s2h, s2l, n1h, n1l, n2h, n2l, f1h, f1l, f2h, f2l,
           eh, el, qh, ql, yh, yl,
           load_sem, send_sem, recv_sem, fin_send, fin_recv):
    me = lax.axis_index("layer")
    core = me % 2
    mate = me + 1 - 2 * core
    half = order // 2
    size = order // PER
    tail = 2 * PER
    device_of, layer_of = placements(n)

    partner, target, source = [], [None], [None]
    for level in range(LEVELS):
        stride = 1 << level
        mine = layer_of[level](me)
        partner.append(device_of[level]((mine + stride * (2 * core - 1) + n) % n))
        target.append(device_of[level + 1](mine))
        source.append(device_of[level](layer_of[level + 1](me)))
    goes_to, comes_from = target[LEVELS], source[LEVELS]
    moves = goes_to != me

    def rows_of(piece, first):
        if isinstance(piece, int) and piece == tail:
            return pl.ds(2 * order, columns)
        which = (piece // PER + first) % 2
        return pl.ds(pl.multiple_of(which * order + (piece % PER) * size, size), size)

    def remote(level, from_slot, to_slot, flow, piece, first, dev):
        return pltpu.make_async_remote_copy(
            src_ref=bufs.at[level, from_slot, rows_of(piece, first)],
            dst_ref=bufs.at[level, to_slot, rows_of(piece, first)],
            send_sem=send_sem.at[level, flow, piece],
            recv_sem=recv_sem.at[level, to_slot - 1, piece],
            device_id=(dev,),
            device_id_type=MESH,
        )

    def hand_on(level, slot, piece):
        remote(level, slot, 3, 2, piece, 1 - core, partner[level]).start()
        remote(level, slot, 2, 1, piece, 1 - core, mate).start()

    def start_own(level, piece):
        remote(level, 0, 1, 0, piece, 1 - target[level] % 2, target[level]).start()

    def send_own(level, piece):
        @pl.when((target[level] != me) & (piece < AHEAD * level))
        def _():
            start_own(level, piece)

        @pl.when(target[level] == me)
        def _():
            hand_on(level, 0, piece)

    barrier = pltpu.get_barrier_semaphore()

    def greet(dev):
        pl.semaphore_signal(barrier, inc=1, device_id=(dev,), device_id_type=MESH)

    loads = []
    for index, (ref, start, count) in enumerate(((upper_ref, 0, order), (lower_ref, order, order), (rhs_ref, 2 * order, columns))):
        copy = pltpu.make_async_copy(ref.at[0], bufs.at[0, 0, pl.ds(start, count)], load_sem.at[index])
        copy.start()
        loads.append(copy)

    greet(mate)
    expected = jnp.int32(1 + LEVELS)
    for level in range(LEVELS):
        greet(partner[level])
    for level in range(1, LEVELS + 1):
        @pl.when(source[level] != me)
        def _():
            greet(source[level])

        expected += (target[level] != me).astype(jnp.int32)
    pl.semaphore_wait(barrier, expected)

    for copy in loads:
        copy.wait()
    for piece in range(tail + 1):
        hand_on(0, 0, piece)

    def block(r):
        return pl.ds(pl.multiple_of(r * half, half), half)

    def split(level, slot, piece, first, high_ref, low_ref):
        high, low = halves(bufs[level, slot, rows_of(piece, first), :])
        rows = pl.ds((piece % PER) * size, size)
        high_ref[rows, :] = high
        low_ref[rows, :] = low

    def store(high_ref, low_ref, rows, value):
        high, low = halves(value)
        high_ref[rows, :] = high
        low_ref[rows, :] = low


    def fin_copy(piece, out, out_rows):
        return pltpu.make_async_remote_copy(
            src_ref=fin.at[rows_of(piece, 0)], dst_ref=out.at[0, out_rows],
            send_sem=fin_send.at[piece], recv_sem=fin_recv.at[piece],
            device_id=(goes_to,), device_id_type=MESH)

    def fin_local(piece, out, out_rows):
        return pltpu.make_async_copy(fin.at[rows_of(piece, 0)], out.at[0, out_rows], load_sem.at[piece])

    def send_fin(piece, out, out_rows):
        @pl.when(moves)
        def _():
            fin_copy(piece, out, out_rows).start()

        @pl.when(jnp.logical_not(moves))
        def _():
            fin_local(piece, out, out_rows).start()

    for level in range(LEVELS):
        if level:
            moved = source[level] != me
            self_slot = jnp.where(moved, 1, 0)
        else:
            moved, self_slot = None, 0
        order_next = 1 - target[level + 1] % 2 if level < LEVELS - 1 else core

        def take_self(piece):
            if moved is not None:
                @pl.when(moved)
                def _():
                    if piece + AHEAD * level <= tail:
                        start_own(level, piece + AHEAD * level)
                    remote(level, 0, 1, 0, piece, 1 - core, mate).wait_recv()
                    hand_on(level, 1, piece)

        def take(slot, piece):
            remote(level, 0, slot, 0, piece, core, mate).wait_recv()

        def take_near(piece):
            take(2, piece)
            split(level, self_slot, piece, 1 - core, *((s1h, s1l) if piece < PER else (s2h, s2l)))
            split(level, 2, piece, core, *((n1h, n1l) if piece < PER else (n2h, n2l)))

        def take_far(piece):
            take(3, piece)
            split(level, 3, piece, core, *((f1h, f1l) if piece < PER else (f2h, f2l)))

        def first_term(r):
            rows = pl.ds(r * half, half)
            acc[rows, :] = dot3(s1h[rows, :], s1l[rows, :], f1h[...], f1l[...])

        def near_coupling(r):
            rows = pl.ds(r * half, half)
            store(xh.at[core], xl.at[core], rows, dot3(s2h[rows, :], s2l[rows, :], n1h[...], n1l[...]))

        def far_coupling(k):
            inner = pl.ds(k * half, half)
            value = dot3(s1h[:, inner], s1l[:, inner], f2h[inner, :], f2l[inner, :])
            if k == 0:
                part[...] = value
            else:
                store(xh.at[1 - core], xl.at[1 - core], pl.ds(0, order), part[...] + value)

        def inverse():
            every = pl.ds(0, order)
            store(eh, el, every, acc[...] + dot3(s2h[...], s2l[...], n2h[...], n2l[...]))
            store(qh, ql, every, dot3(eh[...], el[...], eh[...], el[...]))
            rows = lax.broadcasted_iota(jnp.int32, (order, order), 0)
            cols = lax.broadcasted_iota(jnp.int32, (order, order), 1)
            eye = jnp.where(rows == cols, 1.0, 0.0).astype(F32)
            value = dot3(eh[...], el[...], qh[...], ql[...])
            e = eh[...].astype(F32) + el[...].astype(F32)
            q = qh[...].astype(F32) + ql[...].astype(F32)
            store(yh, yl, every, eye + (e + (q + value)))

        def emit(position):
            which = (position + order_next) % 2

            @pl.loop(0, 2)
            def _(r):
                value = dot3(yh[block(r), :], yl[block(r), :], xh[which], xl[which])
                rows = pl.ds(pl.multiple_of(which * order + r * half, half), half)
                if level < LEVELS - 1:
                    bufs[level + 1, 0, rows, :] = -value
                else:
                    fin[rows, :] = value * (-factor)
                for t in range(PER // 2):
                    at = r * (PER // 2) + t
                    if level < LEVELS - 1:
                        send_own(level + 1, position * PER + at)
                    else:
                        out_rows = pl.ds(pl.multiple_of(at * size, size), size)

                        @pl.when(which == 0)
                        def _():
                            send_fin(at, out_upper, out_rows)

                        @pl.when(which == 1)
                        def _():
                            send_fin(PER + at, out_lower, out_rows)

        if level == 0:
            for piece in range(tail):
                take_near(piece)
            near_coupling(0)
            near_coupling(1)
            for piece in range(PER):
                take_far(piece)
            for r in range(2):
                first_term(r)
            inverse()
            for piece in range(PER, tail - PER // 2):
                take_far(piece)
            far_coupling(0)
            for piece in range(tail - PER // 2, tail):
                take_far(piece)
        else:
            work = {
                PER + LAG - 1: functools.partial(first_term, 0),
                PER + LAG: functools.partial(first_term, 1),
                PER + PER // 2 + LAG - 1: functools.partial(near_coupling, 0),
                PER + PER // 2 + LAG: functools.partial(far_coupling, 0),
            }
            for step in range(tail + 1):
                take_self(step)
                if step >= 1:
                    take_near(step - 1)
                if step >= LAG:
                    take_far(step - LAG)
                if step in work:
                    work[step]()
            inverse()
            near_coupling(1)

        if level == LEVELS - 1:
            emit(0)
        else:
            @pl.when(order_next == core)
            def _():
                emit(0)

        if level:
            for piece in range(tail + 1 - LAG, tail):
                take_far(piece)
        far_coupling(1)
        if level < LEVELS - 1:
            @pl.when(order_next != core)
            def _():
                emit(0)

        emit(1)

        take(2, tail)
        take(3, tail)
        near_high, near_low = halves(bufs[level, 2, rows_of(tail, 0), :])
        far_high, far_low = halves(bufs[level, 3, rows_of(tail, 0), :])
        right = (bufs[level, self_slot, rows_of(tail, 0), :]
                 - dot3(near_high, near_low, s2h[...], s2l[...], True)
                 - dot3(far_high, far_low, s1h[...], s1l[...], True))
        right_high, right_low = halves(right)
        right = dot3(right_high, right_low, yh[...], yl[...], True)
        if level < LEVELS - 1:
            bufs[level + 1, 0, rows_of(tail, 0), :] = right
            send_own(level + 1, tail)
        else:
            fin[rows_of(tail, 0), :] = right
            send_fin(tail, out_rhs, pl.ds(0, columns))

    for level in range(LEVELS):
        for piece in range(tail + 1):
            if level:
                @pl.when(target[level] != me)
                def _():
                    remote(level, 0, 1, 0, piece, core, target[level]).wait_send()
            remote(level, 0, 2, 1, piece, core, mate).wait_send()
            remote(level, 0, 3, 2, piece, core, partner[level]).wait_send()

    ends = [(p, out_lower if p >= PER else out_upper, pl.ds((p % PER) * size, size)) for p in range(tail)]
    ends.append((tail, out_rhs, pl.ds(0, columns)))
    for piece, out, out_rows in ends:
        @pl.when(moves)
        def _():
            copy = fin_copy(piece, out, out_rows)
            copy.wait_send()
            copy.wait_recv()

        @pl.when(jnp.logical_not(moves))
        def _():
            fin_local(piece, out, out_rows).wait()


def settle(*refs):
    sources, results, held, in_sem, out_sem = refs[:3], refs[3:6], refs[6:9], refs[9], refs[10]
    quarters = []
    for part in range(4):
        for which in range(3):
            rows = held[which].shape[1] // 4
            at = pl.ds(part * rows, rows)
            load = pltpu.make_async_copy(sources[which].at[0, at], held[which].at[0, at], in_sem.at[which, part])
            keep = pltpu.make_async_copy(held[which].at[0, at], results[which].at[0, at], out_sem.at[which, part])
            load.start()
            quarters.append((load, keep))
    for load, keep in quarters:
        load.wait()
        keep.start()
    for _, keep in quarters:
        keep.wait()


def per_device(lower_block, upper_block, right_side):
    n = lax.axis_size("layer")
    order, columns = lower_block.shape[2], right_side.shape[1]
    rows = 2 * order + columns
    one = lambda: pltpu.VMEM((order, order), BF16)
    pieces = 2 * PER + 1
    reduced = pl.pallas_call(
        functools.partial(kernel, n, order, columns, 2.5**8 * math.sqrt(order)),
        out_shape=[jax.ShapeDtypeStruct(a.shape, F32) for a in (lower_block, upper_block, right_side)],
        in_specs=[pl.BlockSpec(memory_space=pl.ANY)] * 3,
        out_specs=[pl.BlockSpec(memory_space=pl.ANY)] * 3,
        scratch_shapes=[
            pltpu.VMEM((LEVELS, 4, rows, order), F32),
            pltpu.VMEM((rows, order), F32),
            pltpu.VMEM((order, order), F32),
            pltpu.VMEM((order, order), F32),
            pltpu.VMEM((2, order, order), BF16),
            pltpu.VMEM((2, order, order), BF16),
            *[one() for _ in range(18)],
            pltpu.SemaphoreType.DMA((pieces,)),
            pltpu.SemaphoreType.DMA((LEVELS, 3, pieces)),
            pltpu.SemaphoreType.DMA((LEVELS, 3, pieces)),
            pltpu.SemaphoreType.DMA((pieces,)),
            pltpu.SemaphoreType.DMA((pieces,)),
        ],
        compiler_params=pltpu.CompilerParams(
            collective_id=0, has_side_effects=True, vmem_limit_bytes=60 * 1024 * 1024
        ),
    )(lower_block, upper_block, right_side)
    return pl.pallas_call(
        settle,
        out_shape=[jax.ShapeDtypeStruct(a.shape, F32) for a in reduced],
        in_specs=[pl.BlockSpec(memory_space=pl.ANY)] * 3,
        out_specs=[pl.BlockSpec(memory_space=pl.ANY)] * 3,
        scratch_shapes=[
            *[pltpu.VMEM(a.shape, F32) for a in reduced],
            pltpu.SemaphoreType.DMA((3, 4)),
            pltpu.SemaphoreType.DMA((3, 4)),
        ],
    )(*reduced)


def solution(mesh):
    placed = (P("layer", None, None), P("layer", None, None), P("layer", None, None))
    return jax.shard_map(
        per_device,
        mesh=mesh,
        in_specs=placed,
        out_specs=placed,
        check_vma=False,
    )
```
